32 devices in a mesh: grp: 4 (over y, x), leaf: 8 (over z, core).
Axes of the slice: x: 2, y: 2, z: 4, core: 2. Of those that a mesh axis runs over, the one named last changes fastest.
Arguments:
- basis: float32 [8, 65536], P(None, ('grp', 'leaf')), may hold values from -28 to 28
- roots: float32 [5], replicated, may hold values from 0.35 to 1
- near_blocks: bfloat16 [256, 6, 256, 256], P(('grp', 'leaf')), may hold values from -0.046875 to 0.046875
- near_ids: int32 [256, 6], P(('grp', 'leaf')), may hold values from 0 to 255, as said below
- leaf_basis: bfloat16 [256, 64, 256], P(('grp', 'leaf')), may hold values from -0.375 to 0.375
- far_coupling: bfloat16 [256, 8, 64, 64], P(('grp', 'leaf')), may hold values from -0.109375 to 0.109375
- far_ids: int32 [256, 8], P(('grp', 'leaf')), may hold values from 0 to 255, as said below
- transfer: bfloat16 [256, 64, 128], P(('grp', 'leaf')), may hold values from -0.5 to 0.5
- top_coupling: bfloat16 [128, 8, 128, 128], P(('grp', 'leaf')), may hold values from -0.078125 to 0.078125
- top_ids: int32 [128, 8], P(('grp', 'leaf')), may hold values from 0 to 127, as said below
Outputs:
- next_vector: float32 [65536], P(('grp', 'leaf'))
- hessen: float32 [9], replicated
The draws below stay inside these ranges and needn't reach their ends.
Inputs may be any that keep to these rules, and one draw needn't show every extreme that they name: `near_ids`: row i starts with i itself; the others lie within 8 leaves of i. `far_ids`: every entry lies within 8 leaves of its row. `top_ids`: every entry lies within 4 parents of its row.
All inputs are finite; a program needn't handle non-finite values.
Results may differ from the reference program's by a relative error of at most 0.024.
Values may be sent and summed in bfloat16 or wider, within the bound.
A program may use at most 64 MiB of HBM per device.

```python
import jax
import jax.numpy as jnp
from jax import lax

LEAF = 256
RANK = 64
PRANK = 128
LPD = 8
NEAR = 6
FAR = 8
TOPL = 8
BASIS = 8
ROOTS = 5
LEAVES = 256
PARENTS = 128
PANELS = 65536


def local_ids(key, rows_count, count, reach):
    rows = jnp.arange(rows_count, dtype=jnp.int32)[:, None]
    offsets = jax.random.randint(key, (rows_count, count), -reach, reach + 1)
    return jnp.clip(rows + offsets, 0, rows_count - 1).astype(jnp.int32)


def draw_near_ids(key, part):
    others = local_ids(jax.random.fold_in(key, 11), LEAVES, NEAR - 1, LPD)
    itself = jnp.arange(LEAVES, dtype=jnp.int32)[:, None]
    return jnp.concatenate([itself, others], axis=1).astype(jnp.int32)


def draw_far_ids(key, part):
    return local_ids(jax.random.fold_in(key, 23), LEAVES, FAR, LPD)


def draw_top_ids(key, part):
    return local_ids(jax.random.fold_in(key, 37), PARENTS, TOPL, LPD // 2)


def draw_basis(key, part):
    position = jnp.arange(PANELS, dtype=jnp.float32) / jnp.float32(PANELS)
    rising = jnp.exp2(2.0 * position)
    leaf_scale = jnp.exp(jax.random.uniform(jax.random.fold_in(key, 51), (LEAVES, 1), jnp.float32, jnp.log(0.7), jnp.log(1.4)))
    rough = jnp.broadcast_to(leaf_scale, (LEAVES, LEAF)).reshape(PANELS)
    noise = jnp.clip(jax.random.normal(jax.random.fold_in(key, 53), (BASIS, PANELS), jnp.float32), -4.0, 4.0)
    common = jnp.clip(jax.random.normal(jax.random.fold_in(key, 59), (1, PANELS), jnp.float32), -4.0, 4.0)
    values = noise + 0.4 * common
    return (values * (rising * rough)[None, :]).astype(jnp.float32)


def shard_levels(key, extent, split, low, largest):
    level, own = 1.0, jax.random.fold_in(key, 6)
    for dim, blocks in split:
        draws = jnp.exp(jax.random.uniform(jax.random.fold_in(own, dim), (blocks,), jnp.float32, low / len(split), largest / len(split)))
        level = level * jnp.repeat(draws, extent[dim] // blocks).reshape([-1 if axis == dim else 1 for axis in range(len(extent))])
    return level


def gaussian(rng, extent, scale, bound, split=(), kind=jnp.bfloat16):
    values = scale * jax.random.normal(rng, extent, jnp.float32)
    if split:
        values = values * shard_levels(rng, extent, split, -0.22, 0.18)
    return jnp.clip(values, -bound, bound).astype(kind)


def setup_inputs(seed: int = 0) -> dict:
    seeds = jax.random.split(jax.random.key(seed), 11)
    basis = draw_basis(jax.random.fold_in(seeds[10], 71), 0)
    roots = jnp.clip(jax.random.uniform(seeds[1], (ROOTS,), jnp.float32, 0.35, 1.0), 0.35, 1.0)
    near_blocks = gaussian(seeds[2], (LEAVES, NEAR, LEAF, LEAF), (LEAF * NEAR * 11) ** -0.5, 0.046875, ((0, 32),))
    near_ids = draw_near_ids(jax.random.fold_in(seeds[10], 71), 0)
    leaf_basis = gaussian(seeds[4], (LEAVES, RANK, LEAF), LEAF ** -0.5, 0.375, ((0, 32),))
    far_coupling = gaussian(seeds[5], (LEAVES, FAR, RANK, RANK), (FAR * RANK * 6) ** -0.5, 0.109375, ((0, 32),))
    far_ids = draw_far_ids(jax.random.fold_in(seeds[10], 71), 0)
    transfer = gaussian(seeds[7], (LEAVES, RANK, PRANK), (2 * RANK) ** -0.5, 0.5, ((0, 32),))
    top_coupling = gaussian(seeds[8], (PARENTS, TOPL, PRANK, PRANK), (TOPL * PRANK * 6) ** -0.5, 0.078125, ((0, 32),))
    top_ids = draw_top_ids(jax.random.fold_in(seeds[10], 71), 0)
    return dict(basis=basis, roots=roots, near_blocks=near_blocks, near_ids=near_ids, leaf_basis=leaf_basis, far_coupling=far_coupling, far_ids=far_ids, transfer=transfer, top_coupling=top_coupling, top_ids=top_ids)


def apply_operator(field, near_blocks, near_ids, leaf_basis, far_coupling, far_ids, transfer, top_coupling, top_ids):
    rounded = field.astype(jnp.bfloat16)
    groups = LEAVES // LPD

    def near_piece(pieces):
        blocks, indices = pieces
        nearby = rounded[indices].astype(jnp.float32)
        return jnp.einsum('lkab,lkb->la', blocks.astype(jnp.float32), nearby)
    near_term = lax.map(near_piece, (near_blocks.reshape(groups, LPD, NEAR, LEAF, LEAF), near_ids.reshape(groups, LPD, NEAR)))
    near_term = near_term.reshape(LEAVES, LEAF)
    coeffs = jnp.einsum('lra,la->lr', leaf_basis.astype(jnp.float32), rounded.astype(jnp.float32)).astype(jnp.bfloat16)
    partners = coeffs[far_ids].astype(jnp.float32)
    leaf_sum = jnp.einsum('lkrs,lks->lr', far_coupling.astype(jnp.float32), partners)
    upward = jnp.einsum('lrp,lr->lp', transfer.astype(jnp.float32), coeffs.astype(jnp.float32))
    upward = upward.reshape(PARENTS, 2, PRANK).sum(1).astype(jnp.bfloat16)
    sources = upward[top_ids].astype(jnp.float32)
    top_sum = jnp.einsum('pkab,pkb->pa', top_coupling.astype(jnp.float32), sources).astype(jnp.bfloat16)
    down = jnp.einsum('lrp,lp->lr', transfer.astype(jnp.float32), jnp.repeat(top_sum, 2, axis=0).astype(jnp.float32))
    local_coef = (leaf_sum + down).astype(jnp.bfloat16)
    far_term = jnp.einsum('lra,lr->la', leaf_basis.astype(jnp.float32), local_coef.astype(jnp.float32))
    return 0.5 * field + near_term + far_term

def reference(basis, roots, near_blocks, near_ids, leaf_basis, far_coupling, far_ids, transfer, top_coupling, top_ids):

    def operator(field):
        return apply_operator(field, near_blocks, near_ids, leaf_basis, far_coupling, far_ids, transfer, top_coupling, top_ids)
    vectors = basis.reshape(BASIS, LEAVES, LEAF)
    product = vectors[BASIS - 1]
    result = jnp.zeros_like(product)
    for index in range(ROOTS):
        result = result + product / roots[index]
        if index < ROOTS - 1:
            product = product - operator(product) / roots[index]
    image = operator(result)
    total = jnp.float32(PANELS)
    hcoef = jnp.einsum('mla,la->m', vectors, image, precision=lax.Precision.HIGHEST) / total
    remain = image - jnp.einsum('m,mla->la', hcoef, vectors, precision=lax.Precision.HIGHEST)
    beta = jnp.sqrt(jnp.sum(remain * remain) / total + 1e-06)
    next_vector = (remain / beta).reshape(PANELS)
    hessen = jnp.concatenate([hcoef, beta[None]])
    return (next_vector, hessen)
```

```python
import functools

import jax
import jax.numpy as jnp
from jax import lax
from jax.experimental import pallas as pl
from jax.experimental.pallas import tpu as pltpu
from jax.sharding import PartitionSpec as P

MESH = pl.DeviceIdType.MESH
F32 = jnp.float32
BF16 = jnp.bfloat16


def nt(a, b):
    return lax.dot_general(a, b, (((1,), (1,)), ((), ())), preferred_element_type=F32)


def nn(a, b):
    return lax.dot_general(a, b, (((1,), (0,)), ((), ())), preferred_element_type=F32)


def kernel(
    n_grp,
    n_leaf,
    basis,
    roots,
    near_hbm,
    near_ids,
    lb_hbm,
    fc_hbm,
    far_ids,
    tr_hbm,
    tc_hbm,
    top_ids,
    out,
    hess,
    near,
    lb,
    fc,
    fcc,
    tr,
    tc,
    halo,
    prod_buf,
    z_buf,
    slots,
    load_sem,
    near_sem,
    send_sem,
    recv_sem,
    red_sem,
):
    n_dev = n_grp * n_leaf
    count = basis.shape[0]
    leaves, n_near, width, _ = near.shape
    n_far, rank = fc.shape[1], fc.shape[2]
    n_top, prank = tc.shape[1], tc.shape[2]
    parents = tc.shape[0]
    steps = roots.shape[0]
    coefs = leaves * rank
    me = lax.axis_index("grp") * n_leaf + lax.axis_index("leaf")

    def place(index):
        return (index // n_leaf, index % n_leaf)

    right = lax.rem(me + 1, n_dev)
    left = lax.rem(me + n_dev - 1, n_dev)

    lb_copy = pltpu.make_async_copy(lb_hbm, lb, load_sem.at[0])
    tr_copy = pltpu.make_async_copy(tr_hbm, tr, load_sem.at[1])
    fc_copy = pltpu.make_async_copy(fc_hbm, fc, load_sem.at[2])
    tc_copy = pltpu.make_async_copy(tc_hbm, tc, load_sem.at[3])
    near_copies = [
        pltpu.make_async_copy(near_hbm.at[i], near.at[i], near_sem.at[i]) for i in range(leaves)
    ]
    lb_copy.start()
    tr_copy.start()
    fc_copy.start()
    tc_copy.start()
    for copy in near_copies:
        copy.start()

    barrier = pltpu.get_barrier_semaphore()

    def greet(d, carry):
        pl.semaphore_signal(
            barrier, inc=1, device_id=place(lax.rem(me + d, n_dev)), device_id_type=MESH
        )
        return carry

    lax.fori_loop(1, n_dev, greet, 0)

    for i in range(leaves):
        prod_buf[i : i + 1, :] = basis[count - 1 : count, i * width : (i + 1) * width]
    z_buf[...] = jnp.zeros_like(z_buf)

    def iota(shape, dim):
        return lax.broadcasted_iota(jnp.int32, shape, dim)

    cands = 4 * leaves

    def onehots(columns):
        return [jnp.where(c == iota((leaves, cands), 1), 1.0, 0.0).astype(F32) for c in columns]

    base = me * leaves - leaves
    nid = near_ids[...] - base
    near_hot = jnp.concatenate(onehots([nid[:, k : k + 1] for k in range(1, n_near)]), 0)
    near_hot = near_hot.astype(BF16)
    fid = far_ids[...] - base
    far_hot = jnp.concatenate(onehots([fid[:, k : k + 1] for k in range(n_far)]), 0).astype(BF16)
    base_p = me * parents - parents
    tid = jnp.zeros((leaves, n_top), jnp.int32)
    for p in range(parents):
        tid = jnp.where(iota((leaves, n_top), 0) // 2 == p, top_ids[p : p + 1, :], tid)
    tid = (tid - base_p) * 2
    top_hot = jnp.concatenate(onehots([tid[:, k : k + 1] for k in range(n_top)]), 0).astype(BF16)

    gram = lax.dot_general(
        basis[...],
        basis[...],
        (((1,), (1,)), ((), ())),
        precision=lax.Precision.HIGHEST,
        preferred_element_type=F32,
    )

    row512 = iota((leaves, coefs), 0)
    block512 = iota((leaves, coefs), 1) // rank
    diag = row512 == block512
    row_l = iota((leaves, 2 * rank), 0)
    row_w = iota((leaves, width), 0)
    row_p = iota((leaves, prank), 0)
    low = iota((leaves, 2 * rank), 1) < rank

    fc_copy.wait()
    for k in range(n_far):
        for i in range(leaves):
            fcc[i * rank : (i + 1) * rank, k * rank : (k + 1) * rank] = fc[i, k]
    lb_copy.wait()
    tr_copy.wait()
    pl.semaphore_wait(barrier, n_dev - 1)

    def apply(step, field, first):
        xb = field.astype(BF16)
        full = jnp.where(diag, nt(xb, lb[...]), 0.0)
        part = full[:, 0 : 2 * rank]
        for v in range(1, leaves // 2):
            part = part + full[:, v * 2 * rank : (v + 1) * 2 * rank]
        part = part.astype(BF16).astype(F32)
        dup = part + pltpu.roll(part, rank, 1)
        swapped = jnp.where(
            row_l % 2 == 0, pltpu.roll(part, leaves - 1, 0), pltpu.roll(part, 1, 0)
        )
        pair = part + swapped
        lhs = jnp.concatenate(
            [jnp.where(row_l // 2 == v, pair, 0.0) for v in range(leaves // 2)], 1
        ).astype(BF16)
        up = nn(lhs, tr[...]).astype(BF16).astype(F32)
        halo[step, 1, :, 0:width] = xb.astype(F32)
        halo[step, 1, :, width : width + 2 * rank] = dup
        halo[step, 1, :, width + 2 * rank :] = up
        copies = []
        for side, target in ((0, right), (2, left)):
            copy = pltpu.make_async_remote_copy(
                src_ref=halo.at[step, 1],
                dst_ref=halo.at[step, side],
                send_sem=send_sem.at[step, side // 2],
                recv_sem=recv_sem.at[step, side // 2],
                device_id=place(target),
                device_id_type=MESH,
            )
            copy.start()
            copies.append(copy)
        acc = 0.5 * field
        own = []
        for i in range(leaves):
            if first:
                near_copies[i].wait()
            own.append(nt(xb, near[i, 0]))
        if first:
            tc_copy.wait()
        for copy in copies:
            copy.wait()
        cand = jnp.concatenate(
            [halo[step, 0], halo[step, 1], halo[step, 2], jnp.zeros_like(halo[step, 0])], 0
        ).astype(BF16)
        coef = nn(far_hot, cand[:, width : width + 2 * rank])
        par = nn(top_hot, cand[:, width + 2 * rank :])
        near_x = nn(near_hot, cand[:, 0:width])
        par_k = [par[k * leaves : (k + 1) * leaves].astype(BF16) for k in range(n_top)]
        srow = jnp.zeros((leaves, prank), F32)
        for p in range(parents):
            r = nt(par_k[0], tc[p, 0])
            for k in range(1, n_top):
                r = r + nt(par_k[k], tc[p, k])
            srow = jnp.where(row_p // 2 == p, r, srow)
        far_lhs = jnp.concatenate(
            [
                jnp.where(
                    low,
                    coef[2 * v * leaves : (2 * v + 1) * leaves],
                    coef[(2 * v + 1) * leaves : (2 * v + 2) * leaves],
                )
                for v in range(n_far // 2)
            ],
            1,
        ).astype(BF16)
        leaf_sum = nt(far_lhs, fcc[...])
        down = nt(srow.astype(BF16), tr[...])
        g = jnp.where(diag, leaf_sum + down, 0.0).astype(BF16)
        far = nn(g, lb[...])
        acc = acc + far
        xk = [near_x[k * leaves : (k + 1) * leaves].astype(BF16) for k in range(n_near - 1)]
        for i in range(leaves):
            r = own[i]
            for k in range(1, n_near):
                r = r + nt(xk[k - 1], near[i, k])
            acc = acc + jnp.where(row_w == i, r, 0.0)
        return acc

    def body(step, first):
        root = roots[step]
        prod = prod_buf[...]
        scaled = prod / root
        z = z_buf[...] + scaled
        z_buf[...] = z
        last = step == steps - 1
        field = jnp.where(last, z, prod)
        image = apply(step, field, first)
        prod_buf[...] = jnp.where(last, image, prod - image / root)

    body(0, True)

    def loop(step, carry):
        body(step, False)
        return carry

    lax.fori_loop(1, steps, loop, 0)

    w = prod_buf[...]
    proj = jnp.zeros((count, width), F32)
    for i in range(leaves):
        proj = proj + basis[:, i * width : (i + 1) * width] * w[i : i + 1, :]
    hcol = jnp.sum(proj, 1, keepdims=True)
    wcol = jnp.sum(w * w, 1, keepdims=True)
    lane = iota((count, 128), 1)
    rows = iota((count, 128), 0)
    tile = jnp.where(lane == count, hcol, 0.0) + jnp.where(lane == count + 1, wcol, 0.0)
    tile = tile + jnp.pad(gram, ((0, 0), (0, 128 - count)))
    slots[me] = tile

    def spread(d, carry):
        pltpu.make_async_remote_copy(
            src_ref=slots.at[me],
            dst_ref=slots.at[me],
            send_sem=red_sem.at[0],
            recv_sem=red_sem.at[1],
            device_id=place(lax.rem(me + d, n_dev)),
            device_id_type=MESH,
        ).start()
        return carry

    lax.fori_loop(1, n_dev, spread, 0)
    rest = pltpu.make_async_remote_copy(
        src_ref=slots.at[pl.ds(0, n_dev - 1)],
        dst_ref=slots.at[pl.ds(0, n_dev - 1)],
        send_sem=red_sem.at[0],
        recv_sem=red_sem.at[1],
        device_id=place(right),
        device_id_type=MESH,
    )
    rest.wait_recv()
    total = jnp.sum(slots[...], 0) * (1.0 / (leaves * width * n_dev))
    h = jnp.sum(jnp.where(lane == count, total, 0.0), 1, keepdims=True)
    ww = jnp.sum(jnp.where(lane == count + 1, total, 0.0), keepdims=True)
    hrow = jnp.sum(jnp.where(lane == rows, h, 0.0), 0, keepdims=True)
    quad = jnp.sum(h * (total * hrow), keepdims=True)
    hh = jnp.sum(h * h, keepdims=True)
    squared = jnp.maximum(ww - 2.0 * hh + quad, 0.0)
    beta = jnp.sqrt(squared + 1e-06)
    inverse = 1.0 / beta
    lane1 = iota((1, 128), 1)
    full = jnp.where(lane1 == count, beta, hrow)
    hess[...] = full[:, 0 : count + 1]
    for i in range(leaves):
        fit = jnp.sum(basis[:, i * width : (i + 1) * width] * h, 0, keepdims=True)
        out[:, i * width : (i + 1) * width] = (w[i : i + 1, :] - fit) * inverse
    rest.wait_send()


def make_body(n_grp, n_leaf):
    def body(
        basis,
        roots,
        near_blocks,
        near_ids,
        leaf_basis,
        far_coupling,
        far_ids,
        transfer,
        top_coupling,
        top_ids,
    ):
        leaves, rank, width = leaf_basis.shape
        prank = transfer.shape[2]
        count = basis.shape[0]
        steps = roots.shape[0]
        n_dev = n_grp * n_leaf
        payload = width + 2 * rank + prank
        vmem = pl.BlockSpec(memory_space=pltpu.VMEM)
        smem = pl.BlockSpec(memory_space=pltpu.SMEM)
        hbm = pl.BlockSpec(memory_space=pl.ANY)
        lb = leaf_basis.reshape(leaves * rank, width)
        tr = transfer.reshape(leaves * rank, prank)
        n_far = far_coupling.shape[1]
        out, hess = pl.pallas_call(
            functools.partial(kernel, n_grp, n_leaf),
            out_shape=(
                jax.ShapeDtypeStruct((1, leaves * width), F32),
                jax.ShapeDtypeStruct((1, count + 1), F32),
            ),
            in_specs=[vmem, smem, hbm, vmem, hbm, hbm, vmem, hbm, hbm, vmem],
            out_specs=(vmem, vmem),
            scratch_shapes=[
                pltpu.VMEM(near_blocks.shape, BF16),
                pltpu.VMEM(lb.shape, BF16),
                pltpu.VMEM(far_coupling.shape, BF16),
                pltpu.VMEM((leaves * rank, n_far * rank), BF16),
                pltpu.VMEM(tr.shape, BF16),
                pltpu.VMEM(top_coupling.shape, BF16),
                pltpu.VMEM((steps, 3, leaves, payload), F32),
                pltpu.VMEM((leaves, width), F32),
                pltpu.VMEM((leaves, width), F32),
                pltpu.VMEM((n_dev, count, 128), F32),
                pltpu.SemaphoreType.DMA((4,)),
                pltpu.SemaphoreType.DMA((leaves,)),
                pltpu.SemaphoreType.DMA((steps, 2)),
                pltpu.SemaphoreType.DMA((steps, 2)),
                pltpu.SemaphoreType.DMA((2,)),
            ],
            compiler_params=pltpu.CompilerParams(
                collective_id=0, has_side_effects=True, vmem_limit_bytes=48 * 1024 * 1024
            ),
        )(
            basis,
            roots,
            near_blocks,
            near_ids,
            lb,
            far_coupling,
            far_ids,
            tr,
            top_coupling,
            top_ids,
        )
        return out.reshape(leaves * width), hess.reshape(count + 1)

    return body


def solution(mesh):
    both = ("grp", "leaf")
    return jax.shard_map(
        make_body(mesh.shape["grp"], mesh.shape["leaf"]),
        mesh=mesh,
        in_specs=(
            P(None, both),
            P(),
            P(both, None, None, None),
            P(both, None),
            P(both, None, None),
            P(both, None, None, None),
            P(both, None),
            P(both, None, None),
            P(both, None, None, None),
            P(both, None),
        ),
        out_specs=(P(both), P()),
        check_vma=False,
    )
```
